256 devices in a mesh: seq: 8 (over z_hi, x), head: 32 (over y, z_lo, core).
Axes of the slice: x: 4, y: 4, z: 8 (z_hi: 2, z_lo: 4; z = z_hi * 4 + z_lo), core: 2. Of those that a mesh axis runs over, the one named last changes fastest.
Arguments:
- queries: bfloat16 [8192, 8192], P(('seq', 'head')), may hold values from -6 to 6
- keys: bfloat16 [8192, 8192], P(('seq', 'head')), may hold values from -6 to 6
- values: bfloat16 [8192, 8192], P(('seq', 'head')), may hold values from -6 to 6
- out_grad: bfloat16 [8192, 8192], P(('seq', 'head')), may hold values from -6 to 6
- selected: int32 [64, 16, 3], P('head', 'seq'), may hold values from 0 to 14, as said below
- length: int32 [1], replicated, may hold values from 4096 to 8192
Outputs:
- attended: bfloat16 [8192, 8192], P(('seq', 'head'))
- query_grad: bfloat16 [8192, 8192], P(('seq', 'head'))
- key_grad: bfloat16 [8192, 8192], P(('seq', 'head'))
- value_grad: bfloat16 [8192, 8192], P(('seq', 'head'))
The draws below stay inside these ranges and needn't reach their ends.
Inputs may be any that keep to these rules, and one draw needn't show every extreme that they name: `selected`: for head h and query block b every entry lies in 0 to b; the entries below b are distinct, there are min(3, b) of them, and b-1 is one of them when b > 0; the other entries equal b.
All inputs are finite; a program needn't handle non-finite values.
Results may differ from the reference program's by a relative error of at most 0.012.
The reference program's roundings to bfloat16 on the way (of `weights_low`, `grad_in` and `dscores`) count: a program that leaves them out, or rounds other values in their place, can miss the bound.
Values may be sent and summed in bfloat16 or wider, within the bound.
A program may use at most 128 MiB of HBM per device.

```python
import math
import jax
import jax.numpy as jnp
from jax import lax

HEADS = 64
HD = 128
BLOCK = 512
TOP = 3
TOK_DEV = 1024
TOKENS = 8192
NBLK = 16
N_SEQ = 8


def base_draw(key, salt):
    return jnp.clip(jax.random.normal(jax.random.fold_in(key, salt), (TOKENS, HEADS * HD), jnp.float32), -6.0, 6.0)


def draw_queries(key, part):
    result = base_draw(key, 1)
    return result.astype(jnp.bfloat16)


def draw_keys(key, part):
    result = base_draw(key, 2)
    return result.astype(jnp.bfloat16)


def draw_selected(key, part):
    block_count = TOKENS // BLOCK
    raw = jax.random.randint(key, (HEADS, block_count, block_count), 0, 1 << 20)
    candidate = jnp.arange(block_count, dtype=jnp.int32)[None, None, :]
    query_block = jnp.arange(block_count, dtype=jnp.int32)[None, :, None]
    scores = jnp.where(candidate < query_block, raw * block_count + candidate + 1, -1 - candidate)
    scores = jnp.where(candidate == query_block - 1, jnp.int32(1 << 30), scores)
    best_scores, best_index = jax.lax.top_k(scores, TOP)
    own = jnp.arange(block_count, dtype=jnp.int32)[None, :, None]
    return jnp.where(best_index < own, best_index, own).astype(jnp.int32)


def level_of(own_key, shape, pieces, least, top_value):
    factor_of = 1.0
    for position, parts in pieces:
        heights = jax.random.uniform(jax.random.fold_in(jax.random.fold_in(own_key, 6), position), (parts,), jnp.float32, least / len(pieces), top_value / len(pieces))
        factor_of = factor_of * jnp.repeat(jnp.exp(heights), shape[position] // parts).reshape((-1,) + (1,) * (len(shape) - 1 - position))
    return factor_of


def noise(own_key, shape, spread, bound, shards=(), kind=jnp.bfloat16):
    values = spread * jax.random.normal(own_key, shape, jnp.float32)
    if shards:
        values = values * level_of(own_key, shape, shards, -0.22, 0.18)
    return jnp.clip(values, -bound, bound).astype(kind)


def setup_inputs(seed: int = 0) -> dict:
    splits = jax.random.split(jax.random.key(seed), 7)
    queries = draw_queries(jax.random.fold_in(splits[6], 71), 0)
    keys = draw_keys(jax.random.fold_in(splits[6], 71), 0)
    values = noise(splits[2], (TOKENS, HEADS * HD), 1.0, 6.0, ((0, 256),))
    out_grad = noise(splits[3], (TOKENS, HEADS * HD), 1.0, 6.0, ((0, 256),))
    selected = draw_selected(jax.random.fold_in(splits[6], 71), 0)
    length = jax.random.randint(splits[5], (1,), TOKENS // 2, TOKENS + 1).astype(jnp.int32)
    return dict(queries=queries, keys=keys, values=values, out_grad=out_grad, selected=selected, length=length)


masked_score = -1e+30

def rounded(matrix):
    return lax.optimization_barrier(matrix.astype(jnp.bfloat16)).astype(jnp.float32)

def usable_mask(chosen, block_id, row_count):
    whole = chosen < block_id
    remote = jnp.broadcast_to(whole[:, None], (chosen.shape[0], row_count)).reshape(1, -1)
    remote = jnp.broadcast_to(remote, (row_count, chosen.shape[0] * row_count))
    lower = jnp.arange(row_count)[None, :] <= jnp.arange(row_count)[:, None]
    return jnp.concatenate([remote, lower], axis=1)

def attend(query_rows, key_set, value_set, grad_rows, usable, live_rows):
    scaling = 1.0 / math.sqrt(query_rows.shape[-1])
    scores = jnp.dot(query_rows, key_set.T, preferred_element_type=jnp.float32) * scaling
    scores = jnp.where(usable, scores, masked_score)
    row_max = lax.optimization_barrier(jnp.max(scores, axis=1, keepdims=True))
    raised = jnp.exp(scores - row_max)
    weights = raised / lax.optimization_barrier(jnp.sum(raised, axis=1, keepdims=True))
    weights_low = weights.astype(jnp.bfloat16)
    output = jnp.dot(weights_low, value_set, preferred_element_type=jnp.float32)
    output = jnp.where(live_rows[:, None], output, 0.0).astype(jnp.bfloat16)
    grad_in = jnp.where(live_rows[:, None], grad_rows, jnp.zeros_like(grad_rows))
    dweights = jnp.dot(grad_in, value_set.T, preferred_element_type=jnp.float32)
    delta = lax.optimization_barrier(jnp.sum(grad_in.astype(jnp.float32) * output.astype(jnp.float32), axis=1, keepdims=True))
    dscores = (weights * (dweights - delta) * scaling).astype(jnp.bfloat16)
    query_grad = jnp.dot(dscores, key_set, preferred_element_type=jnp.float32).astype(jnp.bfloat16)
    key_term = jnp.dot(dscores.T, query_rows, preferred_element_type=jnp.float32)
    value_term = jnp.dot(weights_low.T, grad_in, preferred_element_type=jnp.float32)
    return (output, query_grad, key_term, value_term)

def head_pass(head_index, queries, keys, values, out_grad, selected, length):
    start = head_index * HD
    query_head = lax.dynamic_slice_in_dim(queries, start, HD, 1).reshape(NBLK, BLOCK, HD)
    key_head = lax.dynamic_slice_in_dim(keys, start, HD, 1).reshape(NBLK, BLOCK, HD)
    value_head = lax.dynamic_slice_in_dim(values, start, HD, 1).reshape(NBLK, BLOCK, HD)
    grad_head = lax.dynamic_slice_in_dim(out_grad, start, HD, 1).reshape(NBLK, BLOCK, HD)
    chosen_all = lax.dynamic_index_in_dim(selected, head_index, 0, keepdims=False)

    def one_block(block_id):
        chosen = chosen_all[block_id]
        block_list = jnp.concatenate([chosen, block_id[None]]).astype(jnp.int32)
        key_set = key_head[block_list].reshape(-1, HD)
        value_set = value_head[block_list].reshape(-1, HD)
        live_rows = block_id * BLOCK + jnp.arange(BLOCK, dtype=jnp.int32) < length[0]
        return attend(query_head[block_id], key_set, value_set, grad_head[block_id], usable_mask(chosen, block_id, BLOCK), live_rows)
    outputs, query_grads, key_terms, value_terms = lax.map(one_block, jnp.arange(NBLK, dtype=jnp.int32))
    owners = jnp.concatenate([chosen_all, jnp.arange(NBLK, dtype=jnp.int32)[:, None]], 1)
    per_group = TOK_DEV // BLOCK
    key_sum = jnp.zeros((NBLK, BLOCK, HD), jnp.float32)
    value_sum = jnp.zeros((NBLK, BLOCK, HD), jnp.float32)
    for group in range(N_SEQ):
        lower_row = group * per_group
        upper_row = lower_row + per_group
        block_ids = owners[lower_row:upper_row].reshape(-1)
        onehot = (jnp.arange(NBLK, dtype=jnp.int32)[:, None] == block_ids[None, :]).astype(jnp.float32)
        key_group = key_terms[lower_row:upper_row].reshape(-1, BLOCK, HD)
        value_group = value_terms[lower_row:upper_row].reshape(-1, BLOCK, HD)
        key_sum = key_sum + rounded(jnp.einsum('ke,erd->krd', onehot, key_group, precision=lax.Precision.HIGHEST))
        value_sum = value_sum + rounded(jnp.einsum('ke,erd->krd', onehot, value_group, precision=lax.Precision.HIGHEST))
    return (outputs.reshape(TOKENS, HD), query_grads.reshape(TOKENS, HD), key_sum.reshape(TOKENS, HD).astype(jnp.bfloat16), value_sum.reshape(TOKENS, HD).astype(jnp.bfloat16))

def merge_heads(stacked):
    return jnp.transpose(stacked, (1, 0, 2)).reshape(TOKENS, HEADS * HD)

def reference(queries, keys, values, out_grad, selected, length):

    def run_head(head_index):
        return head_pass(head_index, queries, keys, values, out_grad, selected, length)
    results = lax.map(run_head, jnp.arange(HEADS, dtype=jnp.int32))
    return (merge_heads(results[0]), merge_heads(results[1]), merge_heads(results[2]), merge_heads(results[3]))
```

```python
import math

import jax
import jax.numpy as jnp
from jax import lax
from jax.experimental import pallas as pl
from jax.experimental.pallas import tpu as pltpu
from jax.sharding import PartitionSpec as P

HD = 128
BLOCK = 512
TOP = 3
ROWS = 32
HEADS = 64
QUARTER = 2048
TOKENS = 8192
PEERS = 64

NEG = -1e30
SCALE = 1.0 / math.sqrt(HD)
SCALE2 = SCALE * math.log2(math.e)


def place():
    s = lax.axis_index("seq")
    hh = lax.axis_index("head")
    zh, x = lax.div(s, 4), lax.rem(s, 4)
    yz, c = lax.div(hh, 2), lax.rem(hh, 2)
    half = lax.div(x, 2)
    pair = jnp.where(half == 0, x, 3 - x)
    return s, hh, zh, x, yz, c, half, pair


def dev(s, hh):
    return {"seq": s, "head": hh}


def head_holder(h, half, zh):
    pair = lax.rem(lax.div(h, 2), 2)
    x = jnp.where(half == 0, pair, 3 - pair)
    return dev(lax.rem(h, 2) * 4 + x, lax.div(h, 4) * 2 + zh)


def greet(s, hh, zh, x, yz, c, half):
    barrier = pltpu.get_barrier_semaphore()
    mine = h_of()
    own = c == zh

    def to_holder(i, carry):
        @pl.when(jnp.logical_not(jnp.logical_and(own, i == 0)))
        def _():
            pl.semaphore_signal(barrier, inc=1, device_id=head_holder(lax.rem(mine + i, HEADS), half, zh))
        return carry

    def to_owner(i, carry):
        r = lax.rem(lax.rem(x, 2) * 32 + hh + i, PEERS)

        @pl.when(jnp.logical_not(jnp.logical_and(own, i == 0)))
        def _():
            pl.semaphore_signal(barrier, inc=1, device_id=owner_of(r, half, c))
        return carry

    return barrier, to_holder, to_owner


def h_of():
    s, hh, zh, x, yz, c, half, pair = place()
    return 2 * (yz * 2 + pair) + zh


def owner_of(r, half, c):
    return dev(c * 4 + 2 * half + lax.div(r, 32), lax.rem(r, 32))


def mates(s, hh, zh, x, yz, c):
    across = zh * 4 + 3 - x
    return dev(across, hh), dev(s, yz * 2 + 1 - c), dev(across, yz * 2 + 1 - c)


def whole_wait(ref, sem):
    pltpu.make_async_copy(ref, ref, sem).wait()


def gather_kernel(k_ref, v_ref, q_ref, g_ref, sel_ref, k_out, v_out, q_out, g_out, sel_out,
                  own_sem, arrive, left, pass_arrive, pass_left, sel_sem):
    s, hh, zh, x, yz, c, half, pair = place()
    mine = h_of()
    own = c == zh
    barrier, _, to_owner = greet(s, hh, zh, x, yz, c, half)
    lax.fori_loop(0, PEERS, to_owner, 0)
    across, beside, diagonal = mates(s, hh, zh, x, yz, c)
    for mate in (across, beside, diagonal):
        pl.semaphore_signal(barrier, inc=1, device_id=mate)
    pl.semaphore_wait(barrier, PEERS + 3 - own.astype(jnp.int32))

    row_quarter = (lax.rem(x, 2) * 32 + hh) * ROWS
    row_all = (s * 32 + hh) * ROWS

    def scatter(n, src, dst, row):
        row = pl.multiple_of(row, ROWS)

        def one(i, carry):
            h = lax.rem(mine + i, HEADS)
            part = src.at[:, pl.ds(pl.multiple_of(h * HD, HD), HD)]
            there = dst.at[pl.ds(row, ROWS), :]
            keep = jnp.logical_and(own, i == 0)

            @pl.when(keep)
            def _():
                pltpu.make_async_copy(part, there, arrive.at[n]).start()

            @pl.when(jnp.logical_not(keep))
            def _():
                pltpu.make_async_remote_copy(part, there, left.at[n], arrive.at[n],
                                             device_id=head_holder(h, half, zh)).start()
            return carry
        lax.fori_loop(0, PEERS, one, 0)

    for hb in range(2):
        h = 2 * (yz * 2 + c) + hb
        keep = jnp.logical_and(own, jnp.logical_and(hb == zh, c == pair))
        there = sel_out.at[lax.rem(x, 2)]

        @pl.when(keep)
        def _(hb=hb, there=there):
            pltpu.make_async_copy(sel_ref.at[hb], there, sel_sem.at[0]).start()

        @pl.when(jnp.logical_not(keep))
        def _(hb=hb, there=there, h=h):
            pltpu.make_async_remote_copy(sel_ref.at[hb], there, sel_sem.at[1], sel_sem.at[0],
                                         device_id=head_holder(h, half, zh)).start()

    scatter(0, k_ref, k_out, row_all)
    scatter(1, v_ref, v_out, row_all)

    q = c * 2 + half
    outs = (k_out, v_out)

    def region(a, p):
        return outs[a].at[pl.ds(p * QUARTER, QUARTER), :]

    def hand_on(a, p, slot, target):
        return pltpu.make_async_remote_copy(region(a, p), region(a, p), pass_left.at[a, slot],
                                            pass_arrive.at[a, p], device_id=target)

    def quarter_rows(a):
        return outs[a].at[pl.ds(pl.multiple_of(q * QUARTER, QUARTER), QUARTER), :]

    for a in range(2):
        whole_wait(quarter_rows(a), arrive.at[a])

        @pl.when(q == 0)
        def _(a=a):
            hand_on(a, 0, 0, across).start()
            hand_on(a, 0, 1, beside).start()

        @pl.when(q == 1)
        def _(a=a):
            hand_on(a, 1, 0, diagonal).start()
            hand_on(a, 1, 1, beside).start()

        @pl.when(q == 2)
        def _(a=a):
            hand_on(a, 2, 0, across).start()

        if a == 0:
            scatter(2, q_ref, q_out, row_quarter)
            scatter(3, g_ref, g_out, row_quarter)

    for a in range(2):
        @pl.when(q == 1)
        def _(a=a):
            whole_wait(region(a, 0), pass_arrive.at[a, 0])
            hand_on(a, 0, 2, beside).start()

    for a in range(2):
        @pl.when(q >= 2)
        def _(a=a):
            whole_wait(region(a, 0), pass_arrive.at[a, 0])
            whole_wait(region(a, 1), pass_arrive.at[a, 1])

        @pl.when(q == 3)
        def _(a=a):
            whole_wait(region(a, 2), pass_arrive.at[a, 2])
    whole_wait(q_out, arrive.at[2])
    whole_wait(g_out, arrive.at[3])
    whole_wait(sel_out, sel_sem.at[0])

    for a in range(2):
        @pl.when(q == 0)
        def _(a=a):
            whole_wait(region(a, 0), pass_left.at[a, 0])
            whole_wait(region(a, 0), pass_left.at[a, 1])

        @pl.when(q == 1)
        def _(a=a):
            whole_wait(region(a, 1), pass_left.at[a, 0])
            whole_wait(region(a, 1), pass_left.at[a, 1])
            whole_wait(region(a, 0), pass_left.at[a, 2])

        @pl.when(q == 2)
        def _(a=a):
            whole_wait(region(a, 2), pass_left.at[a, 0])
    part = q_out.at[pl.ds(0, QUARTER - ROWS), :]
    last = q_out.at[pl.ds(0, ROWS), :]
    for n in range(4):
        whole_wait(part, left.at[n])

        @pl.when(jnp.logical_not(own))
        def _(n=n):
            whole_wait(last, left.at[n])
    for hb in range(2):
        keep = jnp.logical_and(own, jnp.logical_and(hb == zh, c == pair))

        @pl.when(jnp.logical_not(keep))
        def _(hb=hb):
            whole_wait(sel_ref.at[hb], sel_sem.at[1])


def attend_kernel(sel_ref, info_ref, q_ref, g_ref, k_ref, v_ref, o_ref, dq_ref, dk_ref, dv_ref,
                  dk_acc, dv_acc, st):
    first = info_ref[0]
    length = info_ref[1]
    dk_acc[...] = jnp.zeros_like(dk_acc)
    dv_acc[...] = jnp.zeros_like(dv_acc)
    nt = (((1,), (1,)), ((), ()))
    tn = (((0,), (0,)), ((), ()))

    def rows_of(block):
        return pl.ds(pl.multiple_of(block * BLOCK, BLOCK), BLOCK)

    def one_block(j, carry):
        b = first + j
        rows = rows_of(j)
        q = q_ref[rows, :]
        live = (b * BLOCK + lax.broadcasted_iota(jnp.int32, (BLOCK, 1), 0)) < length
        g = jnp.where(live, g_ref[rows, :], jnp.zeros((), jnp.bfloat16))
        slot_rows = lax.div(j, 2)
        lane = lax.rem(j, 2) * TOP
        ids = [sel_ref[slot_rows, 0, lane + t] for t in range(TOP)] + [b]
        m = jnp.full((1, BLOCK), NEG, jnp.float32)
        for t in range(TOP + 1):
            sc = lax.dot_general(k_ref[rows_of(ids[t]), :], q, nt, preferred_element_type=jnp.float32)
            if t < TOP:
                sc = jnp.where(ids[t] < b, sc, NEG)
            else:
                kv = lax.broadcasted_iota(jnp.int32, (BLOCK, BLOCK), 0)
                qp = lax.broadcasted_iota(jnp.int32, (BLOCK, BLOCK), 1)
                sc = jnp.where(kv <= qp, sc, NEG)
            st[t] = sc
            m = jnp.maximum(m, jnp.max(sc, axis=0, keepdims=True))
        total = jnp.zeros((1, BLOCK), jnp.float32)
        for t in range(TOP + 1):
            p = jnp.exp2((st[t] - m) * SCALE2)
            total = total + jnp.sum(p, axis=0, keepdims=True)
            st[t] = p
        inv = 1.0 / total
        out_t = jnp.zeros((HD, BLOCK), jnp.float32)
        for t in range(TOP + 1):
            w = st[t] * inv
            st[t] = w
            low = w.astype(jnp.bfloat16)
            out_t = out_t + lax.dot_general(v_ref[rows_of(ids[t]), :], low, tn, preferred_element_type=jnp.float32)
            dv_acc[rows_of(ids[t]), :] += jnp.dot(low, g, preferred_element_type=jnp.float32)
        out = jnp.where(live, out_t.T, 0.0).astype(jnp.bfloat16)
        o_ref[rows, :] = out
        delta = jnp.sum((g.astype(jnp.float32) * out.astype(jnp.float32)).T, axis=0, keepdims=True)
        dq_t = jnp.zeros((HD, BLOCK), jnp.float32)
        for t in range(TOP + 1):
            dw = lax.dot_general(v_ref[rows_of(ids[t]), :], g, nt, preferred_element_type=jnp.float32)
            ds = (st[t] * (dw - delta) * SCALE).astype(jnp.bfloat16)
            dq_t = dq_t + lax.dot_general(k_ref[rows_of(ids[t]), :], ds, tn, preferred_element_type=jnp.float32)
            dk_acc[rows_of(ids[t]), :] += jnp.dot(ds, q, preferred_element_type=jnp.float32)
        dq_ref[rows, :] = dq_t.T.astype(jnp.bfloat16)
        return carry

    lax.fori_loop(0, QUARTER // BLOCK, one_block, 0)
    dk_ref[...] = dk_acc[...].astype(jnp.bfloat16)
    dv_ref[...] = dv_acc[...].astype(jnp.bfloat16)


def return_kernel(o_ref, dq_ref, dk_ref, dv_ref, o_out, dq_out, dk_out, dv_out,
                  own_part, near_part, got, relay, final, load_sem,
                  arrive, left, part_arrive, part_left):
    s, hh, zh, x, yz, c, half, pair = place()
    mine = h_of()
    own = c == zh
    q = c * 2 + half
    barrier, to_holder, _ = greet(s, hh, zh, x, yz, c, half)
    lax.fori_loop(0, PEERS, to_holder, 0)
    across, beside, diagonal = mates(s, hh, zh, x, yz, c)
    for mate in (across, beside, diagonal):
        pl.semaphore_signal(barrier, inc=1, device_id=mate)

    parts = (dk_ref, dv_ref)

    def region(a, p):
        return parts[a].at[pl.ds(pl.multiple_of(p * QUARTER, QUARTER), QUARTER), :]

    for a in range(2):
        pltpu.make_async_copy(region(a, q), own_part.at[a], load_sem.at[a]).start()

        @pl.when(q == 1)
        def _(a=a):
            pltpu.make_async_copy(region(a, 0), near_part.at[a], load_sem.at[2 + a]).start()

    pl.semaphore_wait(barrier, PEERS + 3 - own.astype(jnp.int32))

    def send_part(a, p, slot, into, target):
        return pltpu.make_async_remote_copy(region(a, p), got.at[a, into], part_left.at[a, slot],
                                            part_arrive.at[a, into], device_id=target)

    for a in range(2):
        @pl.when(q == 3)
        def _(a=a):
            send_part(a, 0, 0, 2, beside).start()
            send_part(a, 1, 1, 1, beside).start()
            send_part(a, 2, 2, 0, across).start()

        @pl.when(q == 2)
        def _(a=a):
            send_part(a, 0, 0, 1, beside).start()
            send_part(a, 1, 1, 0, diagonal).start()

    start_row = lax.rem(x, 2) * 32 + hh
    column = pl.ds(pl.multiple_of(mine * HD, HD), HD)

    def scatter(n, src, dst):
        def one(i, carry):
            r = lax.rem(start_row + i, PEERS)
            part = src.at[pl.ds(pl.multiple_of(r * ROWS, ROWS), ROWS), :]
            there = dst.at[:, column]
            keep = jnp.logical_and(own, i == 0)

            @pl.when(keep)
            def _():
                pltpu.make_async_copy(part, there, arrive.at[n]).start()

            @pl.when(jnp.logical_not(keep))
            def _():
                pltpu.make_async_remote_copy(part, there, left.at[n], arrive.at[n],
                                             device_id=owner_of(r, half, c)).start()
            return carry
        lax.fori_loop(0, PEERS, one, 0)

    def relay_copy(a):
        return pltpu.make_async_remote_copy(relay.at[a], got.at[a, 0], part_left.at[a, 0],
                                            part_arrive.at[a, 0], device_id=across)

    scatter(0, o_ref, o_out)

    @pl.when(q == 1)
    def _():
        for a in range(2):
            pltpu.make_async_copy(region(a, 0), near_part.at[a], load_sem.at[2 + a]).wait()
            whole_wait(got.at[a, 2], part_arrive.at[a, 2])
            relay[a] = (near_part[a].astype(jnp.float32) + got[a, 2].astype(jnp.float32)).astype(jnp.bfloat16)
            relay_copy(a).start()

    scatter(1, dq_ref, dq_out)

    for a in range(2):
        pltpu.make_async_copy(region(a, q), own_part.at[a], load_sem.at[a]).wait()

        @pl.when(q < 2)
        def _(a=a):
            whole_wait(got.at[a, 0], part_arrive.at[a, 0])
            whole_wait(got.at[a, 1], part_arrive.at[a, 1])
            final[a] = (own_part[a].astype(jnp.float32) + got[a, 0].astype(jnp.float32)
                        + got[a, 1].astype(jnp.float32)).astype(jnp.bfloat16)

        @pl.when(q == 2)
        def _(a=a):
            whole_wait(got.at[a, 0], part_arrive.at[a, 0])
            final[a] = (own_part[a].astype(jnp.float32) + got[a, 0].astype(jnp.float32)).astype(jnp.bfloat16)

        @pl.when(q == 3)
        def _(a=a):
            final[a] = own_part[a]
        scatter(2 + a, final.at[a], dk_out if a == 0 else dv_out)

    for n, out in enumerate((o_out, dq_out, dk_out, dv_out)):
        whole_wait(out, arrive.at[n])
    for a in range(2):
        @pl.when(q == 3)
        def _(a=a):
            for slot in range(3):
                whole_wait(got.at[a, 0], part_left.at[a, slot])

        @pl.when(q == 2)
        def _(a=a):
            for slot in range(2):
                whole_wait(got.at[a, 0], part_left.at[a, slot])

        @pl.when(q == 1)
        def _(a=a):
            whole_wait(got.at[a, 0], part_left.at[a, 0])
    part = final.at[0, pl.ds(0, QUARTER - ROWS), :]
    last = final.at[0, pl.ds(0, ROWS), :]
    for n in range(4):
        whole_wait(part, left.at[n])

        @pl.when(jnp.logical_not(own))
        def _(n=n):
            whole_wait(last, left.at[n])


ANY = pl.BlockSpec(memory_space=pl.ANY)
VMEM = pl.BlockSpec(memory_space=pltpu.VMEM)
SMEM = pl.BlockSpec(memory_space=pltpu.SMEM)


def body(queries, keys, values, out_grad, selected, length):
    low = jnp.bfloat16
    shape = jax.ShapeDtypeStruct
    dma = pltpu.SemaphoreType.DMA
    padded = jnp.pad(selected.reshape(2, 1, 2 * TOP), ((0, 0), (0, 7), (0, 128 - 2 * TOP)))
    k_all, v_all, q_here, g_here, sel = pl.pallas_call(
        gather_kernel,
        out_shape=(shape((TOKENS, HD), low), shape((TOKENS, HD), low), shape((QUARTER, HD), low),
                   shape((QUARTER, HD), low), shape((2, 8, 128), jnp.int32)),
        in_specs=[ANY] * 5,
        out_specs=(ANY,) * 5,
        scratch_shapes=[dma((1,)), dma((4,)), dma((4,)), dma((2, 3)), dma((2, 3)), dma((2,))],
        compiler_params=pltpu.CompilerParams(collective_id=0, has_side_effects=True),
        name="gather",
    )(keys, values, queries, out_grad, padded)

    s, hh, zh, x, yz, c, half, pair = place()
    first = (c * 2 + half) * (QUARTER // BLOCK)
    info = jnp.stack([first, length[0]]).astype(jnp.int32)
    o, dq, dk, dv = pl.pallas_call(
        attend_kernel,
        out_shape=(shape((QUARTER, HD), low), shape((QUARTER, HD), low),
                   shape((TOKENS, HD), low), shape((TOKENS, HD), low)),
        in_specs=[SMEM, SMEM, VMEM, VMEM, VMEM, VMEM],
        out_specs=(VMEM,) * 4,
        scratch_shapes=[pltpu.VMEM((TOKENS, HD), jnp.float32), pltpu.VMEM((TOKENS, HD), jnp.float32),
                        pltpu.VMEM((TOP + 1, BLOCK, BLOCK), jnp.float32)],
        compiler_params=pltpu.CompilerParams(vmem_limit_bytes=60 * 1024 * 1024),
        name="attend",
    )(sel, info, q_here, g_here, k_all, v_all)

    owned = shape((ROWS, HEADS * HD), low)
    return pl.pallas_call(
        return_kernel,
        out_shape=(owned,) * 4,
        in_specs=[ANY] * 4,
        out_specs=(ANY,) * 4,
        scratch_shapes=[pltpu.VMEM((2, QUARTER, HD), low), pltpu.VMEM((2, QUARTER, HD), low),
                        pltpu.VMEM((2, 3, QUARTER, HD), low), pltpu.VMEM((2, QUARTER, HD), low),
                        pltpu.VMEM((2, QUARTER, HD), low), dma((4,)), dma((4,)), dma((4,)),
                        dma((2, 3)), dma((2, 3))],
        compiler_params=pltpu.CompilerParams(collective_id=1, has_side_effects=True,
                                             vmem_limit_bytes=32 * 1024 * 1024),
        name="give_back",
    )(o, dq, dk, dv)


def solution(mesh):
    rows = P(("seq", "head"), None)
    return jax.shard_map(
        body,
        mesh=mesh,
        in_specs=(rows, rows, rows, rows, P("head", "seq", None), P()),
        out_specs=(rows, rows, rows, rows),
        check_vma=False,
    )
```

```python
import math

import jax
import jax.numpy as jnp
from jax import lax
from jax.experimental import pallas as pl
from jax.experimental.pallas import tpu as pltpu
from jax.sharding import PartitionSpec as P

HD = 128
BLOCK = 512
TOP = 3
ROWS = 32
HEADS = 64
QUARTER = 2048
TOKENS = 8192
PEERS = 64

NEG = -1e30
SCALE = 1.0 / math.sqrt(HD)
SCALE2 = SCALE * math.log2(math.e)


def place():
    s = lax.axis_index("seq")
    hh = lax.axis_index("head")
    zh, x = lax.div(s, 4), lax.rem(s, 4)
    yz, c = lax.div(hh, 2), lax.rem(hh, 2)
    half = lax.div(x, 2)
    pair = jnp.where(half == 0, x, 3 - x)
    return s, hh, zh, x, yz, c, half, pair


def dev(s, hh):
    return {"seq": s, "head": hh}


def head_holder(h, half, zh):
    pair = lax.rem(lax.div(h, 2), 2)
    x = jnp.where(half == 0, pair, 3 - pair)
    return dev(lax.rem(h, 2) * 4 + x, lax.div(h, 4) * 2 + zh)


def h_of():
    s, hh, zh, x, yz, c, half, pair = place()
    return 2 * (yz * 2 + pair) + zh


def owner_of(r, half, c):
    return dev(c * 4 + 2 * half + lax.div(r, 32), lax.rem(r, 32))


def whole_wait(ref, sem):
    pltpu.make_async_copy(ref, ref, sem).wait()


NT = (((1,), (1,)), ((), ()))
TN = (((0,), (0,)), ((), ()))
SLOTS = TOP + 1
NB = QUARTER // BLOCK
NBLK = TOKENS // BLOCK


def fused_kernel(k_ref, v_ref, q_ref, g_ref, chosen_ref, length_ref,
                 o_out, dq_out, dk_out, dv_out,
                 k_all, v_all, q_buf, g_buf, o_buf, dq_buf, sel_own, sel_buf, sel,
                 weights, terms, part, got, relay, final,
                 arrive, left, pass_arrive, pass_left, sel_sem, arrive_out, left_out, part_arrive, part_left):
    s, hh, zh, x, yz, c, half, pair = place()
    mine = h_of()
    own = c == zh
    q = c * 2 + half
    first = q * NB
    across_seq = zh * 4 + 3 - x
    across, beside, diagonal = dev(across_seq, hh), dev(s, yz * 2 + 1 - c), dev(across_seq, yz * 2 + 1 - c)
    start_row = lax.rem(x, 2) * 32 + hh

    barrier = pltpu.get_barrier_semaphore()

    def hello(i, carry):
        r = lax.rem(start_row + i, PEERS)

        @pl.when(jnp.logical_not(jnp.logical_and(own, i == 0)))
        def _():
            pl.semaphore_signal(barrier, inc=1, device_id=owner_of(r, half, c))
        return carry
    lax.fori_loop(0, PEERS, hello, 0)
    for mate in (across, beside, diagonal):
        pl.semaphore_signal(barrier, inc=1, device_id=mate)

    lane = lax.broadcasted_iota(jnp.int32, (8, 128), 1)
    for hb in range(2):
        packed = jnp.zeros((8, 128), jnp.int32)
        for bb in range(2):
            for t in range(TOP):
                packed = jnp.where(lane == bb * TOP + t, chosen_ref[hb, bb, t], packed)
        sel_own[hb] = packed
    pl.semaphore_wait(barrier, PEERS + 3 - own.astype(jnp.int32))

    def scatter(n, src, there):

        def one(i, carry):
            h = lax.rem(mine + i, HEADS)
            piece = src.at[:, pl.ds(pl.multiple_of(h * HD, HD), HD)]
            keep = jnp.logical_and(own, i == 0)

            @pl.when(keep)
            def _():
                pltpu.make_async_copy(piece, there, arrive.at[n]).start()

            @pl.when(jnp.logical_not(keep))
            def _():
                pltpu.make_async_remote_copy(piece, there, left.at[n], arrive.at[n],
                                             device_id=head_holder(h, half, zh)).start()
            return carry
        lax.fori_loop(0, PEERS, one, 0)

    per_block = BLOCK // ROWS
    block_here = 2 * s + lax.div(hh, per_block)
    rows_here = pl.ds(pl.multiple_of(lax.rem(hh, per_block) * ROWS, ROWS), ROWS)
    rows_quarter = pl.ds(pl.multiple_of(start_row * ROWS, ROWS), ROWS)
    scatter(0, k_ref, k_all.at[block_here, rows_here, :])
    scatter(1, v_ref, v_all.at[block_here, rows_here, :])

    def sel_keep(hb):
        return jnp.logical_and(own, jnp.logical_and(hb == zh, c == pair))

    for hb in range(2):
        there = sel_buf.at[lax.rem(x, 2)]

        @pl.when(sel_keep(hb))
        def _(hb=hb, there=there):
            pltpu.make_async_copy(sel_own.at[hb], there, sel_sem.at[0]).start()

        @pl.when(jnp.logical_not(sel_keep(hb)))
        def _(hb=hb, there=there):
            pltpu.make_async_remote_copy(sel_own.at[hb], there, sel_sem.at[1], sel_sem.at[0],
                                         device_id=head_holder(2 * (yz * 2 + c) + hb, half, zh)).start()

    alls = (k_all, v_all)

    def region(a, p):
        return alls[a].at[pl.ds(p * NB, NB)]

    def hand_on(a, p, slot, target):
        return pltpu.make_async_remote_copy(region(a, p), region(a, p), pass_left.at[a, slot],
                                            pass_arrive.at[a, p], device_id=target)

    for a in range(2):
        whole_wait(alls[a].at[pl.ds(first, NB)], arrive.at[a])

        @pl.when(q == 0)
        def _(a=a):
            hand_on(a, 0, 0, across).start()
            hand_on(a, 0, 1, beside).start()

        @pl.when(q == 1)
        def _(a=a):
            hand_on(a, 1, 0, diagonal).start()
            hand_on(a, 1, 1, beside).start()

        @pl.when(q == 2)
        def _(a=a):
            hand_on(a, 2, 0, across).start()

        if a == 0:
            scatter(2, q_ref, q_buf.at[rows_quarter, :])
            scatter(3, g_ref, g_buf.at[rows_quarter, :])

    for a in range(2):
        @pl.when(q == 1)
        def _(a=a):
            whole_wait(region(a, 0), pass_arrive.at[a, 0])
            hand_on(a, 0, 2, beside).start()

    whole_wait(sel_buf, sel_sem.at[0])
    to_scalars = pltpu.make_async_copy(sel_buf, sel, sel_sem.at[2])
    to_scalars.start()
    for a in range(2):
        @pl.when(q >= 2)
        def _(a=a):
            whole_wait(region(a, 0), pass_arrive.at[a, 0])
            whole_wait(region(a, 1), pass_arrive.at[a, 1])

        @pl.when(q == 3)
        def _(a=a):
            whole_wait(region(a, 2), pass_arrive.at[a, 2])
    to_scalars.wait()
    whole_wait(q_buf, arrive.at[2])

    def rows_of(block):
        return pl.ds(pl.multiple_of(block * BLOCK, BLOCK), BLOCK)

    def chosen(j):
        return [sel[lax.div(j, 2), 0, lax.rem(j, 2) * TOP + t] for t in range(TOP)] + [first + j]

    def live_rows(j):
        at = (first + j) * BLOCK + lax.broadcasted_iota(jnp.int32, (BLOCK, HD), 0)
        return jnp.clip(length_ref[0] - at, 0, 1).astype(jnp.float32)

    def usable(ids, b, t):
        return jnp.minimum(b - ids[t], 1)

    def forward(j, carry):
        b = first + j
        ids = chosen(j)
        queries = q_buf[rows_of(j), :]
        tops = []
        for t in range(SLOTS):
            sc = lax.dot_general(k_all[ids[t]], queries, NT, preferred_element_type=jnp.float32)
            if t == TOP:
                kv = lax.broadcasted_iota(jnp.int32, (BLOCK, BLOCK), 0)
                qp = lax.broadcasted_iota(jnp.int32, (BLOCK, BLOCK), 1)
                sc = jnp.where(kv <= qp, sc, NEG)
            weights[j, t] = sc
            top = jnp.max(sc, axis=0, keepdims=True)
            tops.append(top if t == TOP else top + (1 - usable(ids, b, t)).astype(jnp.float32) * NEG)
        m = jnp.maximum(jnp.maximum(tops[0], tops[1]), jnp.maximum(tops[2], tops[3]))
        total = jnp.zeros((1, BLOCK), jnp.float32)
        for t in range(SLOTS):
            shift = m if t == TOP else m - (1 - usable(ids, b, t)).astype(jnp.float32) * NEG
            p = jnp.exp2((weights[j, t] - shift) * SCALE2)
            total = total + jnp.sum(p, axis=0, keepdims=True)
            weights[j, t] = p
        inv = 1.0 / total
        out_t = jnp.zeros((HD, BLOCK), jnp.float32)
        for t in range(SLOTS):
            w = weights[j, t] * inv
            weights[j, t] = w
            out_t = out_t + lax.dot_general(v_all[ids[t]], w.astype(jnp.bfloat16), TN,
                                            preferred_element_type=jnp.float32)
        o_buf[rows_of(j), :] = (out_t.T * live_rows(j)).astype(jnp.bfloat16)
        return carry
    lax.fori_loop(0, NB, forward, 0)

    column = pl.ds(pl.multiple_of(mine * HD, HD), HD)

    def give(n, src, dst, count, row_at):
        def one(i, carry):
            r = row_at(i)
            piece = src.at[pl.ds(pl.multiple_of(r * ROWS, ROWS), ROWS), :]
            there = dst.at[:, column]
            keep = jnp.logical_and(own, r == start_row)

            @pl.when(keep)
            def _():
                pltpu.make_async_copy(piece, there, arrive_out.at[n]).start()

            @pl.when(jnp.logical_not(keep))
            def _():
                pltpu.make_async_remote_copy(piece, there, left_out.at[n], arrive_out.at[n],
                                             device_id=owner_of(r, half, c)).start()
            return carry
        lax.fori_loop(0, count, one, 0)

    def all_rows(i):
        return lax.rem(start_row + i, PEERS)

    whole_wait(g_buf, arrive.at[3])
    give(0, o_buf, o_out, PEERS, all_rows)

    def grad_of(j):
        return (g_buf[rows_of(j), :].astype(jnp.float32) * live_rows(j)).astype(jnp.bfloat16)

    def value_terms(j, carry):
        g = grad_of(j)
        for t in range(SLOTS):
            terms[j * SLOTS + t] = jnp.dot(weights[j, t].astype(jnp.bfloat16), g, preferred_element_type=jnp.float32)
        return carry

    def combine(a, p):
        def one(i, carry):
            kb = p * NB + i
            acc = jnp.zeros((BLOCK, HD), jnp.float32)
            for j in range(NB):
                ids = chosen(j)
                at = NB * SLOTS
                for t in range(SLOTS):
                    apart = jnp.minimum(jnp.maximum(ids[t] - kb, kb - ids[t]), 1)
                    hit = 1 - apart
                    if t < TOP:
                        hit = hit * usable(ids, first + j, t)
                    at = at + hit * (j * SLOTS + t - NB * SLOTS)
                acc = acc + terms[jnp.clip(at, 0, NB * SLOTS)]
            part[a, rows_of(kb), :] = acc.astype(jnp.bfloat16)
            return carry
        lax.fori_loop(0, NB, one, 0)

    def piece_of(a, p):
        return part.at[a, pl.ds(p * QUARTER, QUARTER), :]

    def send_part(a, p, slot, into, target):
        return pltpu.make_async_remote_copy(piece_of(a, p), got.at[a, into], part_left.at[a, slot],
                                            part_arrive.at[a, into], device_id=target)

    def reduce_out(a):
        for p in range(NB):
            @pl.when(p <= q)
            def _(a=a, p=p):
                combine(a, p)
            if p >= 1:
                @pl.when(q == 3)
                def _(a=a, p=p):
                    into, target = ((2, beside), (1, beside), (0, across))[p - 1]
                    send_part(a, p - 1, p - 1, into, target).start()
                if p <= 2:
                    @pl.when(q == 2)
                    def _(a=a, p=p):
                        into, target = ((1, beside), (0, diagonal))[p - 1]
                        send_part(a, p - 1, p - 1, into, target).start()

    def relay_sum(a):
        whole_wait(got.at[a, 2], part_arrive.at[a, 2])
        relay[a] = (part[a, 0:QUARTER, :].astype(jnp.float32) + got[a, 2].astype(jnp.float32)).astype(jnp.bfloat16)

    def relay_send(a):
        pltpu.make_async_remote_copy(relay.at[a], got.at[a, 0], part_left.at[a, 0],
                                     part_arrive.at[a, 0], device_id=across).start()

    terms[NB * SLOTS] = jnp.zeros((BLOCK, HD), jnp.float32)
    lax.fori_loop(0, NB, value_terms, 0)
    reduce_out(1)

    def backward(j, carry):
        ids = chosen(j)
        g = grad_of(j)
        queries = q_buf[rows_of(j), :]
        delta = jnp.sum((g.astype(jnp.float32) * o_buf[rows_of(j), :].astype(jnp.float32)).T, axis=0, keepdims=True)
        dq_t = jnp.zeros((HD, BLOCK), jnp.float32)
        for t in range(SLOTS):
            dw = lax.dot_general(v_all[ids[t]], g, NT, preferred_element_type=jnp.float32)
            ds = (weights[j, t] * (dw - delta) * SCALE).astype(jnp.bfloat16)
            dq_t = dq_t + lax.dot_general(k_all[ids[t]], ds, TN, preferred_element_type=jnp.float32)
            terms[j * SLOTS + t] = jnp.dot(ds, queries, preferred_element_type=jnp.float32)
        dq_buf[rows_of(j), :] = dq_t.T.astype(jnp.bfloat16)

        @pl.when(jnp.logical_and(q == 1, j == 0))
        def _():
            relay_sum(1)

        @pl.when(jnp.logical_and(q == 1, j == 1))
        def _():
            relay_send(1)

        @pl.when(j >= 1)
        def _():
            give(1, dq_buf, dq_out, per_block, lambda i: (j - 1) * per_block + lax.rem(hh + i, per_block))
        return carry
    lax.fori_loop(0, NB, backward, 0)
    reduce_out(0)
    give(1, dq_buf, dq_out, per_block, lambda i: (NB - 1) * per_block + lax.rem(hh + i, per_block))

    @pl.when(q == 1)
    def _():
        relay_sum(0)

    def finish(a):
        own_rows = pl.ds(pl.multiple_of(q * QUARTER, QUARTER), QUARTER)

        @pl.when(q < 2)
        def _():
            whole_wait(got.at[a, 0], part_arrive.at[a, 0])
            whole_wait(got.at[a, 1], part_arrive.at[a, 1])
            final[a] = (part[a, own_rows, :].astype(jnp.float32) + got[a, 0].astype(jnp.float32)
                        + got[a, 1].astype(jnp.float32)).astype(jnp.bfloat16)

        @pl.when(q == 2)
        def _():
            whole_wait(got.at[a, 0], part_arrive.at[a, 0])
            final[a] = (part[a, own_rows, :].astype(jnp.float32) + got[a, 0].astype(jnp.float32)).astype(jnp.bfloat16)

        @pl.when(q == 3)
        def _():
            final[a] = part[a, own_rows, :]

    finish(1)

    @pl.when(q == 1)
    def _():
        relay_send(0)
    give(3, final.at[1], dv_out, PEERS, all_rows)
    finish(0)
    give(2, final.at[0], dk_out, PEERS, all_rows)

    for n, out in enumerate((o_out, dq_out, dk_out, dv_out)):
        whole_wait(out, arrive_out.at[n])
    for a in range(2):
        for where, sems in ((0, (pass_left.at[a, 0], pass_left.at[a, 1])),
                            (1, (pass_left.at[a, 0], pass_left.at[a, 1], pass_left.at[a, 2], part_left.at[a, 0])),
                            (2, (pass_left.at[a, 0], part_left.at[a, 0], part_left.at[a, 1])),
                            (3, (part_left.at[a, 0], part_left.at[a, 1], part_left.at[a, 2]))):
            @pl.when(q == where)
            def _(sems=sems):
                for sem in sems:
                    whole_wait(q_buf, sem)
    most = q_buf.at[pl.ds(0, QUARTER - ROWS), :]
    last = q_buf.at[pl.ds(0, ROWS), :]
    for sems in (left, left_out):
        for n in range(4):
            whole_wait(most, sems.at[n])

            @pl.when(jnp.logical_not(own))
            def _(n=n, sems=sems):
                whole_wait(last, sems.at[n])
    for hb in range(2):
        @pl.when(jnp.logical_not(sel_keep(hb)))
        def _(hb=hb):
            whole_wait(sel_own.at[hb], sel_sem.at[1])


ANY = pl.BlockSpec(memory_space=pl.ANY)
SMEM = pl.BlockSpec(memory_space=pltpu.SMEM)


def body(queries, keys, values, out_grad, selected, length):
    low = jnp.bfloat16
    dma = pltpu.SemaphoreType.DMA
    vmem = pltpu.VMEM
    owned = jax.ShapeDtypeStruct((ROWS, HEADS * HD), low)
    return pl.pallas_call(
        fused_kernel,
        out_shape=(owned,) * 4,
        in_specs=[ANY] * 4 + [SMEM] * 2,
        out_specs=(ANY,) * 4,
        scratch_shapes=[vmem((NBLK, BLOCK, HD), low), vmem((NBLK, BLOCK, HD), low)] + [vmem((QUARTER, HD), low)] * 4
        + [vmem((2, 8, 128), jnp.int32), vmem((2, 8, 128), jnp.int32), pltpu.SMEM((2, 8, 128), jnp.int32),
           vmem((NB, SLOTS, BLOCK, BLOCK), jnp.float32), vmem((NB * SLOTS + 1, BLOCK, HD), jnp.float32),
           vmem((2, TOKENS, HD), low), vmem((2, 3, QUARTER, HD), low), vmem((2, QUARTER, HD), low),
           vmem((2, QUARTER, HD), low),
           dma((4,)), dma((4,)), dma((2, 3)), dma((2, 3)), dma((3,)), dma((4,)), dma((4,)), dma((2, 3)), dma((2, 3))],
        compiler_params=pltpu.CompilerParams(collective_id=0, has_side_effects=True,
                                             vmem_limit_bytes=60 * 1024 * 1024),
        name="fused",
    )(keys, values, queries, out_grad, selected, length)


def solution(mesh):
    rows = P(("seq", "head"), None)
    return jax.shard_map(
        body,
        mesh=mesh,
        in_specs=(rows, rows, rows, rows, P("head", "seq", None), P()),
        out_specs=(rows, rows, rows, rows),
        check_vma=False,
    )
```
